32 devices in a mesh: groups: 2 (over y), tm: 4 (over z), zoom: 2 (over x), pol: 2 (over core).
Axes of the slice: x: 2, y: 2, z: 4, core: 2. Of those that a mesh axis runs over, the one named last changes fastest.
Arguments:
- voltages: bfloat16 [2, 4, 7464960], P('pol', 'groups', ('tm', 'zoom')), parts along dimension 1, may hold values from -6 to 6
- section1_taps: float32 [12, 512], replicated, may hold values from -0.078125 to 0.078125
- section2_taps: float32 [5, 3456], replicated, may hold values from -0.046875 to 0.046875
- band_starts: int32 [4], P('groups'), parts along dimension 0, may hold values from 0 to 511
- band_widths: int32 [4], P('groups'), parts along dimension 0, may hold values from 1 to 20, 24 in all
Outputs:
- fine: float32 [2, 2, 4, 1, 58320], P('pol', 'zoom', 'groups', None, 'tm'), parts along dimension 2
The draws below stay inside these ranges and needn't reach their ends.
There are 2 independent parts, one for each index of `groups`. The reference program is written for one: setup_inputs(seed, part) draws one part's arguments, and reference() takes and returns one part's arrays. A program takes and returns all parts, laid end to end along the dimension named above; an argument that names none is the same for every part. Nothing has to cross between parts.
Inputs may be any that keep to these rules, and one draw needn't show every extreme that they name: `band_widths`: the 2 widths sum to 24, and one band has exactly 20 coarse channels.
All inputs are finite; a program needn't handle non-finite values.
Results may differ from the reference program's by a relative error of at most 0.0069.
Values may be sent and summed in bfloat16 or wider, within the bound.
A program may use at most 192 MiB of HBM per device.

```python
import math
import jax
import jax.numpy as jnp
import numpy as np
from jax import lax

CHAN = 512
HOP = 432
TAPS1 = 12
TAPS2 = 5
FA = 27
FB = 128
FINE = 3456
KEEP = 2916
EDGE = 128
FSPEC = 1
NB = 2
WMAX = 20
LIVE_TOTAL = 24
SPEC_ALL = 17280
SAMPLES = 7464960
POLS = 2


def levels(own_key, extent, shards, smallest, largest):
    factor_of, own = 1.0, jax.random.fold_in(own_key, 6)
    for dim, shards_of in shards:
        heights = jnp.exp(jax.random.uniform(jax.random.fold_in(own, dim), (shards_of,), jnp.float32, smallest / len(shards), largest / len(shards)))
        factor_of = factor_of * jnp.repeat(heights, extent[dim] // shards_of).reshape([-1 if axis == dim else 1 for axis in range(len(extent))])
    return factor_of


def split_up(count, total, bound, skew):
    loads = [(1 << 20) // math.isqrt(standing ** skew) + 1 for standing in range(2, count + 1)]
    surplus, counts = total - bound - (count - 1), [1] * (count - 1)
    while surplus > 0:
        free = [i for i in range(count - 1) if counts[i] < bound]
        whole, remaining = sum([loads[i] for i in free]), surplus
        for i in free:
            more = min(bound - counts[i], max(1, remaining * loads[i] // whole), surplus)
            counts[i] = counts[i] + more
            surplus = surplus - more
    return np.array([bound] + counts)


def uneven(key, amount, total, bound, lean):
    if amount == 2:
        one = jax.random.randint(key, (), max(1, total - bound), min(bound, total - 1) + 1)
        return jnp.stack([one, total - one])
    lengths = jnp.asarray(split_up(amount, total, bound, lean), jnp.int32)
    couples = (amount - 1) // 2
    donor, taker = lengths[1:1 + 2 * couples:2], lengths[2:2 + 2 * couples:2]
    slack = jnp.minimum(donor - 1, bound - taker)
    moved = jax.random.randint(jax.random.fold_in(key, 1), (couples,), 0, 1 << 20) % (slack + 1)
    lengths = lengths.at[1:1 + 2 * couples:2].set(donor - moved).at[2:2 + 2 * couples:2].set(taker + moved)
    return lengths[jax.random.permutation(jax.random.fold_in(key, 2), amount)]


def scatter_about(stream_key, extent, width, bound, cuts=(), held_as=jnp.bfloat16):
    array = width * jax.random.normal(stream_key, extent, jnp.float32)
    if cuts:
        array = array * levels(stream_key, extent, cuts, -0.22, 0.18)
    return jnp.clip(array, -bound, bound).astype(held_as)


def setup_inputs(seed: int = 0, part: int = 0) -> dict:
    key_list = jax.random.split(jax.random.key(seed), 6)
    part_splits = jax.random.split(jax.random.fold_in(key_list[5], part), 6)
    return {
        "voltages": scatter_about(part_splits[0], (POLS, 2, SAMPLES), 1.0, 6.0, ((0, 2), (2, 8))),
        "section1_taps": scatter_about(key_list[1], (TAPS1, CHAN), (TAPS1 * CHAN) ** -0.5, 0.078125, (), jnp.float32),
        "section2_taps": scatter_about(key_list[2], (TAPS2, FINE), (TAPS2 * FINE) ** -0.5, 0.046875, (), jnp.float32),
        "band_starts": jax.random.randint(part_splits[3], (NB,), 0, CHAN).astype(jnp.int32),
        "band_widths": uneven(part_splits[4], NB, LIVE_TOTAL, WMAX, 2).astype(jnp.int32),
    }


def angle_table(rows, cols, length):
    product = (jnp.arange(rows, dtype=jnp.int32)[:, None] * jnp.arange(cols, dtype=jnp.int32)[None, :]) % length
    return product.astype(jnp.float32) * (2.0 * math.pi / length)


def rotation_block(length):
    angles = angle_table(length, length, length)
    cosine_tab = jnp.cos(angles).astype(jnp.bfloat16)
    sine_tab = jnp.sin(angles).astype(jnp.bfloat16)
    return jnp.stack([jnp.stack([cosine_tab, sine_tab]), jnp.stack([-sine_tab, cosine_tab])])


def joined_table(length):
    angles = angle_table(length, length, length)
    cosine_tab = jnp.cos(angles).astype(jnp.bfloat16)
    sine_tab = jnp.sin(angles).astype(jnp.bfloat16)
    top_rows = jnp.concatenate([cosine_tab, -sine_tab], axis=1)
    bottom_rows = jnp.concatenate([sine_tab, cosine_tab], axis=1)
    return jnp.concatenate([top_rows, bottom_rows], axis=0)


def bin_index(radix_a, radix_b, keep_len, edge_len):
    fine_len = radix_a * radix_b
    offsets = (np.arange(keep_len + 2 * edge_len) - keep_len // 2 - edge_len) % fine_len
    base = (offsets % radix_a) * (2 * radix_b) + offsets // radix_a
    return base, base + radix_b


def frame_view(segment, spectra, chan_len, hop_len):
    pieces = -(-chan_len // hop_len)
    framed = segment[:, :(spectra + pieces - 1) * hop_len].reshape(segment.shape[0], spectra + pieces - 1, hop_len)
    joined = jnp.concatenate([framed[:, offset:offset + spectra] for offset in range(pieces)], axis=2)
    return joined[:, :, :chan_len]


def weighted_frames(signal, taps, spectra, hop_len):
    chan_len = taps.shape[1]
    running = jnp.zeros((2, spectra, chan_len), jnp.float32)
    for tap_index in range(taps.shape[0]):
        frames = frame_view(signal[:, tap_index * chan_len:], spectra, chan_len, hop_len)
        running = running + taps[tap_index][None, None, :] * frames.astype(jnp.float32)
    return running.astype(jnp.bfloat16)


def fine_spectra(series, section2_taps, radix_a, radix_b, keep_len, edge_len):
    tap_count, fine_len = section2_taps.shape
    items = series.shape[1]
    row_count = series.shape[2] // fine_len
    spectra = row_count - tap_count + 1
    row_blocks = series.reshape(2, items, row_count, fine_len)
    running = jnp.zeros((2, items, spectra, fine_len), jnp.float32)
    for tap_index in range(tap_count):
        running = running + section2_taps[tap_index] * row_blocks[:, :, tap_index:tap_index + spectra].astype(jnp.float32)
    weighted = running.astype(jnp.bfloat16).reshape(2, items, spectra, radix_a, radix_b)
    partial_value = jnp.einsum("pqkm,qcfmb->pcfkb", rotation_block(radix_a).astype(jnp.float32), weighted.astype(jnp.float32), precision=lax.Precision.HIGHEST)
    angles = angle_table(radix_a, radix_b, fine_len)
    cosine_tab = jnp.cos(angles)
    sine_tab = jnp.sin(angles)
    real_part = partial_value[0] * cosine_tab + partial_value[1] * sine_tab
    imag_part = partial_value[1] * cosine_tab - partial_value[0] * sine_tab
    twiddled = jnp.concatenate([real_part, imag_part], axis=-1).astype(jnp.bfloat16)
    spectrum = jnp.einsum("cfkm,mj->cfkj", twiddled.astype(jnp.float32), joined_table(radix_b).astype(jnp.float32), precision=lax.Precision.HIGHEST)
    flattened = spectrum.reshape(items, spectra, radix_a * 2 * radix_b)
    real_index, imag_index = bin_index(radix_a, radix_b, keep_len, edge_len)
    return jnp.stack([jnp.take(flattened, real_index, axis=2), jnp.take(flattened, imag_index, axis=2)])


def stitch_bands(extended, upper_rim, lower_rim, slot_ids, band_width, keep_len, edge_len):
    centre = extended[..., edge_len:edge_len + keep_len]
    live = (slot_ids < band_width).astype(jnp.float32)[None, :, None, None]
    upper_ok = (slot_ids + 1 < band_width).astype(jnp.float32)[None, :, None, None]
    lower_ok = ((slot_ids >= 1) & (slot_ids < band_width)).astype(jnp.float32)[None, :, None, None]
    ramp = (jnp.arange(edge_len, dtype=jnp.float32) + 0.5) / (2.0 * edge_len)
    upper_weight = ramp * upper_ok
    lower_weight = ramp[::-1] * lower_ok
    low_part = centre[..., :edge_len] * (1.0 - lower_weight) + lower_rim * lower_weight
    high_part = centre[..., keep_len - edge_len:] * (1.0 - upper_weight) + upper_rim * upper_weight
    joined = jnp.concatenate([low_part, centre[..., edge_len:keep_len - edge_len], high_part], axis=-1)
    return joined * live


def reference(voltages, section1_taps, section2_taps, band_starts, band_widths):
    chan_len = section1_taps.shape[1]
    pieces = -(-chan_len // HOP)
    rotation = rotation_block(chan_len).astype(jnp.float32)
    slot_ids = jnp.arange(WMAX, dtype=jnp.int32)
    results = []
    for pol_index in range(POLS):
        signal = jnp.pad(voltages[pol_index], ((0, 0), (0, TAPS1 * chan_len + pieces * HOP)))
        weighted = weighted_frames(signal, section1_taps, SPEC_ALL, HOP)
        coarse = jnp.einsum("pqkn,qsn->pks", rotation, weighted.astype(jnp.float32), precision=lax.Precision.HIGHEST).astype(jnp.bfloat16)

        def one_band(pair):
            start, band_width = pair
            channels = ((start + slot_ids) % chan_len).astype(jnp.int32)
            series = jnp.take(coarse, channels, axis=1)
            extended = fine_spectra(series, section2_taps, FA, FB, KEEP, EDGE)
            zero_rim = jnp.zeros_like(extended[:, :1, :, :EDGE])
            upper_rim = jnp.concatenate([extended[:, 1:, :, :EDGE], zero_rim], axis=1)
            lower_rim = jnp.concatenate([zero_rim, extended[:, :-1, :, KEEP + EDGE:]], axis=1)
            stitched = stitch_bands(extended, upper_rim, lower_rim, slot_ids, band_width, KEEP, EDGE)
            return jnp.transpose(stitched, (0, 2, 1, 3)).reshape(2, FSPEC, WMAX * KEEP)

        results.append(lax.map(one_band, (band_starts, band_widths)))
    return jnp.stack(results)
```

```python
import functools
import math

import jax
import jax.numpy as jnp
import numpy as np
from jax import lax
from jax.experimental import pallas as pl
from jax.experimental.pallas import tpu as pltpu
from jax.sharding import PartitionSpec as P

HOP = 432
FA = 27
FB = 128
KEEP = 2916
EDGE = 128
CH_DEV = 5


def shifted(value, axis, steps):
    count = lax.axis_size(axis)
    initial, last = (max(0, -steps), min(count, count - steps))
    return lax.ppermute(value, axis, [(source, source + steps) for source in range(initial, last)])


def angle_table(rows, cols, length):
    product = (
        jnp.arange(rows, dtype=jnp.int32)[:, None]
        * jnp.arange(cols, dtype=jnp.int32)[None, :]
        % length
    )
    return product.astype(jnp.float32) * (2.0 * math.pi / length)


def rotation_block(length):
    angles = angle_table(length, length, length)
    cosine_tab = jnp.cos(angles).astype(jnp.bfloat16)
    sine_tab = jnp.sin(angles).astype(jnp.bfloat16)
    return jnp.stack([jnp.stack([cosine_tab, sine_tab]), jnp.stack([-sine_tab, cosine_tab])])


def joined_table(length):
    angles = angle_table(length, length, length)
    cosine_tab = jnp.cos(angles).astype(jnp.bfloat16)
    sine_tab = jnp.sin(angles).astype(jnp.bfloat16)
    top_rows = jnp.concatenate([cosine_tab, -sine_tab], axis=1)
    bottom_rows = jnp.concatenate([sine_tab, cosine_tab], axis=1)
    return jnp.concatenate([top_rows, bottom_rows], axis=0)


def frame_view(segment, spectra, chan_len, hop_len):
    pieces = -(-chan_len // hop_len)
    framed = segment[:, : (spectra + pieces - 1) * hop_len].reshape(
        segment.shape[0], spectra + pieces - 1, hop_len
    )
    joined = jnp.concatenate(
        [framed[:, offset : offset + spectra] for offset in range(pieces)], axis=2
    )
    return joined[:, :, :chan_len]


def weighted_frames(signal, taps, spectra, hop_len):
    chan_len = taps.shape[1]
    running = jnp.zeros((2, spectra, chan_len), jnp.float32)
    for tap_index in range(taps.shape[0]):
        frames = frame_view(signal[:, tap_index * chan_len :], spectra, chan_len, hop_len)
        running = running + taps[tap_index][None, None, :] * frames.astype(jnp.float32)
    return running.astype(jnp.bfloat16)


def fine_spectra(series, section2_taps, radix_a, radix_b, keep_len, edge_len):
    tap_count, fine_len = section2_taps.shape
    items = series.shape[1]
    row_count = series.shape[2] // fine_len
    spectra = row_count - tap_count + 1
    row_blocks = series.reshape(2, items, row_count, fine_len)
    running = jnp.zeros((2, items, spectra, fine_len), jnp.float32)
    for tap_index in range(tap_count):
        running = running + section2_taps[tap_index] * row_blocks[
            :, :, tap_index : tap_index + spectra
        ].astype(jnp.float32)
    weighted = running.astype(jnp.bfloat16).reshape(2, items, spectra, radix_a, radix_b)
    partial_value = jnp.einsum(
        "pqkm,qcfmb->pcfkb", rotation_block(radix_a), weighted, preferred_element_type=jnp.float32
    )
    angles = angle_table(radix_a, radix_b, fine_len)
    cosine_tab = jnp.cos(angles)
    sine_tab = jnp.sin(angles)
    real_part = partial_value[0] * cosine_tab + partial_value[1] * sine_tab
    imag_part = partial_value[1] * cosine_tab - partial_value[0] * sine_tab
    twiddled = jnp.concatenate([real_part, imag_part], axis=-1).astype(jnp.bfloat16)
    table = joined_table(radix_b).reshape(2 * radix_b, 2, radix_b)
    spectrum = jnp.einsum(
        "cfkm,mpq->pcfqk", twiddled, table, preferred_element_type=jnp.float32
    ).reshape(2, items, spectra, fine_len)
    first = (-(keep_len // 2) - edge_len) % fine_len
    rest = keep_len + 2 * edge_len - (fine_len - first)
    return jnp.concatenate([spectrum[..., first:], spectrum[..., :rest]], axis=-1)


def stitch_bands(extended, upper_rim, lower_rim, slot_ids, band_width, keep_len, edge_len):
    centre = extended[..., edge_len : edge_len + keep_len]
    live = (slot_ids < band_width).astype(jnp.float32)[None, :, None, None]
    upper_ok = (slot_ids + 1 < band_width).astype(jnp.float32)[None, :, None, None]
    lower_ok = ((slot_ids >= 1) & (slot_ids < band_width)).astype(jnp.float32)[None, :, None, None]
    ramp = (jnp.arange(edge_len, dtype=jnp.float32) + 0.5) / (2.0 * edge_len)
    upper_weight = ramp * upper_ok
    lower_weight = ramp[::-1] * lower_ok
    low_part = centre[..., :edge_len] * (1.0 - lower_weight) + lower_rim * lower_weight
    high_part = centre[..., keep_len - edge_len :] * (1.0 - upper_weight) + upper_rim * upper_weight
    joined = jnp.concatenate(
        [low_part, centre[..., edge_len : keep_len - edge_len], high_part], axis=-1
    )
    return joined * live


GROUP = 8
CHUNK = 1152


def bank_kernel(turns, halves, per_row, x_ref, taps_ref, rot_ref, out_ref, bank, total):
    step = pl.program_id(0)
    half = rot_ref.shape[1] // 2
    chans = half // GROUP
    rot_len = rot_ref.shape[0]
    piece = 128
    lane = lax.broadcasted_iota(jnp.int32, (piece, half), 1) // chans

    @pl.when(step == 0)
    def _():
        total[...] = jnp.zeros_like(total)

    @pl.loop(0, CHUNK // piece)
    def _(part):
        row = pl.multiple_of(part * piece, piece)
        turn = pl.multiple_of((step * CHUNK + row) % rot_len, piece)
        taps = taps_ref[pl.ds(row, piece), :]
        wide = jnp.broadcast_to(taps[:, 0:1], (piece, half))
        for phase in range(1, GROUP):
            wide = jnp.where(lane == phase, taps[:, phase : phase + 1], wide)
        for tab in range(2):
            cols = pl.ds(tab * half, half)
            bank[pl.ds(row, piece), cols] = (
                wide * rot_ref[pl.ds(turn, piece), cols]
            ).astype(jnp.bfloat16)

    shift = step // per_row
    total[shift] += jnp.dot(x_ref[...], bank[...], preferred_element_type=jnp.float32)

    @pl.when(step == pl.num_programs(0) - 1)
    def _():
        rows = out_ref.shape[1]
        real = jnp.zeros((rows, half), jnp.float32)
        imag = jnp.zeros((rows, half), jnp.float32)
        for shift in range(turns):
            upper, lower = pl.ds(shift, rows), pl.ds(halves + shift, rows)
            real += total[shift, upper, :half] + total[shift, lower, half:]
            imag += total[shift, lower, :half] - total[shift, upper, half:]
        out_ref[0] = real.astype(jnp.bfloat16)
        out_ref[1] = imag.astype(jnp.bfloat16)


def slot_bank(signal, taps, channels, spectra):
    tap_count, chan_len = taps.shape
    row_len = GROUP * HOP
    rows = -(-spectra // GROUP)
    reach = (GROUP - 1) * HOP + tap_count * chan_len
    steps = -(-reach // CHUNK)
    per_row = row_len // CHUNK
    turns = -(-steps // per_row)
    halves = -(-(rows + turns - 1) // 16) * 16
    keep = -(-rows // 16) * 16
    if keep + turns - 1 > halves:
        halves += 16
    fill = halves * row_len - signal.shape[1]
    data = jnp.pad(signal, ((0, 0), (0, fill))).reshape(2 * halves, row_len)
    flat = taps.reshape(-1)
    spread = jnp.stack(
        [
            jnp.pad(flat, (phase * HOP, steps * CHUNK - flat.shape[0] - phase * HOP))
            for phase in range(GROUP)
        ],
        axis=1,
    )
    chans = channels.shape[0]
    places = (
        jnp.arange(chan_len, dtype=jnp.int32)[:, None]
        - HOP * jnp.arange(GROUP, dtype=jnp.int32)[None, :]
    ) % chan_len
    places = jnp.repeat(places, chans, axis=1)
    turns_of = places * jnp.tile(channels, GROUP)[None, :] % chan_len
    angles = turns_of.astype(jnp.float32) * (2.0 * math.pi / chan_len)
    rot = jnp.concatenate([jnp.cos(angles), jnp.sin(angles)], axis=1)
    rot = rot.astype(jnp.bfloat16).astype(jnp.float32)
    half = GROUP * chans
    out = pl.pallas_call(
        functools.partial(bank_kernel, turns, halves, per_row),
        grid=(steps,),
        in_specs=[
            pl.BlockSpec((2 * halves, CHUNK), lambda i: (0, i % per_row)),
            pl.BlockSpec((CHUNK, GROUP), lambda i: (i, 0)),
            pl.BlockSpec((chan_len, 2 * half), lambda i: (0, 0)),
        ],
        out_specs=pl.BlockSpec((2, keep, half), lambda i: (0, 0, 0)),
        out_shape=jax.ShapeDtypeStruct((2, keep, half), jnp.bfloat16),
        scratch_shapes=[
            pltpu.VMEM((CHUNK, 2 * half), jnp.bfloat16),
            pltpu.VMEM((turns, 2 * halves, 2 * half), jnp.float32),
        ],
        name="slot_bank",
    )(data, spread, rot)
    out = out[:, :rows].reshape(2, rows, GROUP, chans)
    return jnp.transpose(out, (0, 3, 1, 2)).reshape(2, chans, rows * GROUP)[:, :, :spectra]


def on_device(voltages, section1_taps, section2_taps, band_starts, band_widths):
    signal = voltages[0]
    tap_count, chan_len = section1_taps.shape
    spectra = signal.shape[1] // HOP
    rim_len = tap_count * chan_len - HOP
    tm_count = lax.axis_size("tm")
    zoom_count = lax.axis_size("zoom")
    device_count = tm_count * zoom_count
    slot_count = tm_count * CH_DEV
    following = shifted(signal[:, :rim_len], ("tm", "zoom"), -1)
    offsets = np.arange(-1, CH_DEV + 1)
    slots = np.clip(np.arange(tm_count)[:, None] * CH_DEV + offsets[None, :], 0, slot_count - 1)
    wanted = slots[:, None, :] + slot_count * np.arange(zoom_count)[None, :, None]
    wanted = wanted.reshape(device_count, CH_DEV + 2)
    all_slots = jnp.arange(slot_count, dtype=jnp.int32)
    channels = ((band_starts[:, None] + all_slots[None, :]) % chan_len).reshape(-1)
    if channels.shape[0] <= 48:
        joined = jnp.concatenate([signal, following], axis=1)
        width = -(-channels.shape[0] // 16) * 16
        padded = jnp.pad(channels, (0, width - channels.shape[0]))
        coarse = slot_bank(joined, section1_taps, padded, spectra)
        packed = jnp.stack(
            [
                jnp.stack([coarse[:, int(index)] for index in wanted[:, place]], axis=1)
                for place in range(CH_DEV + 2)
            ],
            axis=1,
        )
    else:
        pieces = -(-chan_len // HOP)
        padded = jnp.concatenate(
            [signal, following, jnp.zeros((2, pieces * HOP), jnp.bfloat16)], axis=1
        )
        weighted = weighted_frames(padded, section1_taps, spectra, HOP)
        coarse = jnp.einsum(
            "pqkn,qsn->pks", rotation_block(chan_len), weighted, preferred_element_type=jnp.float32
        ).astype(jnp.bfloat16)
        order = channels[wanted.T.reshape(-1)]
        packed = jnp.take(coarse, order, axis=1).reshape(2, CH_DEV + 2, device_count, spectra)
    received = lax.all_to_all(packed, ("tm", "zoom"), split_axis=2, concat_axis=2, tiled=True)
    series = received.reshape(2, CH_DEV + 2, -1)
    spans = fine_spectra(series, section2_taps, FA, FB, KEEP, EDGE)
    slot_ids = lax.axis_index("tm") * CH_DEV + jnp.arange(CH_DEV, dtype=jnp.int32)
    band_ids = jnp.arange(band_widths.shape[0], dtype=jnp.int32)
    band_width = jnp.sum(jnp.where(band_ids == lax.axis_index("zoom"), band_widths, 0))
    upper_rim = spans[:, 2:, :, :EDGE]
    lower_rim = spans[:, :CH_DEV, :, KEEP + EDGE :]
    extended = spans[:, 1 : CH_DEV + 1]
    stitched = stitch_bands(extended, upper_rim, lower_rim, slot_ids, band_width, KEEP, EDGE)
    fine_count = stitched.shape[2]
    result = jnp.transpose(stitched, (0, 2, 1, 3)).reshape(2, fine_count, CH_DEV * KEEP)
    return result[None, None]


def solution(mesh):
    placed = (P("pol", "groups", ("tm", "zoom")), P(), P(), P("groups"), P("groups"))
    return jax.shard_map(
        on_device,
        mesh=mesh,
        in_specs=placed,
        out_specs=P("pol", "zoom", "groups", None, "tm"),
        check_vma=False,
    )
```

```python
import functools
import math

import jax
import jax.numpy as jnp
import numpy as np
from jax import lax
from jax.experimental import pallas as pl
from jax.experimental.pallas import tpu as pltpu
from jax.sharding import PartitionSpec as P

HOP = 432
FA = 27
FB = 128
KEEP = 2916
EDGE = 128
CH_DEV = 5


def shifted(value, axis, steps):
    count = lax.axis_size(axis)
    initial, last = (max(0, -steps), min(count, count - steps))
    return lax.ppermute(value, axis, [(source, source + steps) for source in range(initial, last)])


def angle_table(rows, cols, length):
    product = (
        jnp.arange(rows, dtype=jnp.int32)[:, None]
        * jnp.arange(cols, dtype=jnp.int32)[None, :]
        % length
    )
    return product.astype(jnp.float32) * (2.0 * math.pi / length)


def rotation_block(length):
    angles = angle_table(length, length, length)
    cosine_tab = jnp.cos(angles).astype(jnp.bfloat16)
    sine_tab = jnp.sin(angles).astype(jnp.bfloat16)
    return jnp.stack([jnp.stack([cosine_tab, sine_tab]), jnp.stack([-sine_tab, cosine_tab])])


def frame_view(segment, spectra, chan_len, hop_len):
    pieces = -(-chan_len // hop_len)
    framed = segment[:, : (spectra + pieces - 1) * hop_len].reshape(
        segment.shape[0], spectra + pieces - 1, hop_len
    )
    joined = jnp.concatenate(
        [framed[:, offset : offset + spectra] for offset in range(pieces)], axis=2
    )
    return joined[:, :, :chan_len]


def weighted_frames(signal, taps, spectra, hop_len):
    chan_len = taps.shape[1]
    running = jnp.zeros((2, spectra, chan_len), jnp.float32)
    for tap_index in range(taps.shape[0]):
        frames = frame_view(signal[:, tap_index * chan_len :], spectra, chan_len, hop_len)
        running = running + taps[tap_index][None, None, :] * frames.astype(jnp.float32)
    return running.astype(jnp.bfloat16)


def natural_order(series, section2_taps, radix_a, radix_b):
    tap_count, fine_len = section2_taps.shape
    items = series.shape[1]
    row_count = series.shape[2] // fine_len
    spectra = row_count - tap_count + 1
    row_blocks = series.reshape(2, items, row_count, fine_len)
    running = jnp.zeros((2, items, spectra, fine_len), jnp.float32)
    for tap_index in range(tap_count):
        running = running + section2_taps[tap_index] * row_blocks[
            :, :, tap_index : tap_index + spectra
        ].astype(jnp.float32)
    weighted = running.astype(jnp.bfloat16).reshape(2, items, spectra, radix_a, radix_b)
    return weighted, np.arange(radix_b)


def phase_order(received, section2_taps, radix_a, radix_b):
    tap_count, fine_len = section2_taps.shape
    sources, _, lines, rows = received.shape
    items = lines // GROUP
    short = fine_len // GROUP
    row_count = sources * rows // short
    spectra = row_count - tap_count + 1
    lanes = jnp.transpose(received, (1, 2, 0, 3)).reshape(2, items, GROUP, row_count, short)
    taps = jnp.transpose(section2_taps.reshape(tap_count, short, GROUP), (0, 2, 1))
    running = jnp.zeros((2, items, GROUP, spectra, short), jnp.float32)
    for tap_index in range(tap_count):
        running = running + taps[tap_index][:, None, :] * lanes[
            :, :, :, tap_index : tap_index + spectra
        ].astype(jnp.float32)
    inner = radix_b // GROUP
    weighted = running.astype(jnp.bfloat16).reshape(2, items, GROUP, spectra, radix_a, inner)
    weighted = jnp.transpose(weighted, (0, 1, 3, 4, 2, 5)).reshape(
        2, items, spectra, radix_a, radix_b
    )
    order = (np.arange(GROUP)[:, None] + GROUP * np.arange(inner)[None, :]).reshape(-1)
    return weighted, order


def ordered_angles(rows, order, length):
    product = (np.arange(rows)[:, None] * order[None, :] % length).astype(np.float32)
    return jnp.asarray(product) * (2.0 * math.pi / length)


def fine_spectra(weighted, order, keep_len, edge_len):
    _, items, spectra, radix_a, radix_b = weighted.shape
    fine_len = radix_a * radix_b
    partial_value = jnp.einsum(
        "pqkm,qcfmb->pcfkb", rotation_block(radix_a), weighted, preferred_element_type=jnp.float32
    )
    angles = ordered_angles(radix_a, order, fine_len)
    cosine_tab = jnp.cos(angles)
    sine_tab = jnp.sin(angles)
    real_part = partial_value[0] * cosine_tab + partial_value[1] * sine_tab
    imag_part = partial_value[1] * cosine_tab - partial_value[0] * sine_tab
    twiddled = jnp.concatenate([real_part, imag_part], axis=-1).astype(jnp.bfloat16)
    turned = ordered_angles(radix_b, order, radix_b).T
    cosine_b = jnp.cos(turned).astype(jnp.bfloat16)
    sine_b = jnp.sin(turned).astype(jnp.bfloat16)
    table = jnp.concatenate(
        [jnp.stack([cosine_b, -sine_b], axis=1), jnp.stack([sine_b, cosine_b], axis=1)], axis=0
    )
    spectrum = jnp.einsum(
        "cfkm,mpq->pcfqk", twiddled, table, preferred_element_type=jnp.float32
    ).reshape(2, items, spectra, fine_len)
    first = (-(keep_len // 2) - edge_len) % fine_len
    rest = keep_len + 2 * edge_len - (fine_len - first)
    return jnp.concatenate([spectrum[..., first:], spectrum[..., :rest]], axis=-1)


def stitch_bands(extended, upper_rim, lower_rim, slot_ids, band_width, keep_len, edge_len):
    centre = extended[..., edge_len : edge_len + keep_len]
    live = (slot_ids < band_width).astype(jnp.float32)[None, :, None, None]
    upper_ok = (slot_ids + 1 < band_width).astype(jnp.float32)[None, :, None, None]
    lower_ok = ((slot_ids >= 1) & (slot_ids < band_width)).astype(jnp.float32)[None, :, None, None]
    ramp = (jnp.arange(edge_len, dtype=jnp.float32) + 0.5) / (2.0 * edge_len)
    upper_weight = ramp * upper_ok
    lower_weight = ramp[::-1] * lower_ok
    low_part = centre[..., :edge_len] * (1.0 - lower_weight) + lower_rim * lower_weight
    high_part = centre[..., keep_len - edge_len :] * (1.0 - upper_weight) + upper_rim * upper_weight
    joined = jnp.concatenate(
        [low_part, centre[..., edge_len : keep_len - edge_len], high_part], axis=-1
    )
    return joined * live


GROUP = 8
CHUNK = 1152


def bank_kernel(turns, per_row, picks, x_ref, rim_ref, taps_ref, rot_ref, out_ref, data, bank, total, mix):
    step = pl.program_id(0)
    rows = x_ref.shape[1]
    halves = data.shape[0] // 2
    base = halves - rim_ref.shape[1]
    half = rot_ref.shape[1] // 2
    rot_len = rot_ref.shape[0]
    piece = 128

    @pl.when(step == 0)
    def _():
        total[...] = jnp.zeros_like(total)

    for part in range(2):
        data[pl.ds(part * halves, rows), :] = x_ref[part]
        data[pl.ds(part * halves + base, halves - base), :] = rim_ref[part]

    @pl.loop(0, CHUNK // piece)
    def _(index):
        row = pl.multiple_of(index * piece, piece)
        turn = pl.multiple_of((step * CHUNK + row) % rot_len, piece)
        wide = jnp.transpose(jnp.tile(taps_ref[:, pl.ds(row, piece)], (piece // GROUP, 1)))
        for col in range(0, 2 * half, piece):
            bank[pl.ds(row, piece), pl.ds(col, piece)] = (
                wide * rot_ref[pl.ds(turn, piece), pl.ds(col, piece)]
            ).astype(jnp.bfloat16)

    total[step // per_row] += jnp.dot(data[...], bank[...], preferred_element_type=jnp.float32)

    @pl.when(step == pl.num_programs(0) - 1)
    def _():
        for shift in range(1, turns):
            for part in range(2):
                total[shift, pl.ds(part * halves + rows, shift), :] = total[
                    shift, pl.ds(part * halves + base, shift), :
                ]
        for part in range(2):
            whole = jnp.zeros((rows, half), jnp.float32)
            for shift in range(turns):
                upper = total[shift, pl.ds(shift, rows), pl.ds(part * half, half)]
                lower = total[shift, pl.ds(halves + shift, rows), pl.ds((1 - part) * half, half)]
                whole += upper + lower if part == 0 else lower - upper
            mix[pl.ds(0, rows), :] = whole
            turned = jnp.transpose(mix[...])
            for dest, pick in enumerate(picks):
                out_ref[dest, part] = turned[
                    pick * GROUP : pick * GROUP + out_ref.shape[2], :rows
                ].astype(jnp.bfloat16)


def slot_bank(signal, following, taps, channels, spectra, picks, width):
    tap_count, chan_len = taps.shape
    row_len = GROUP * HOP
    rows = spectra // GROUP
    reach = (GROUP - 1) * HOP + tap_count * chan_len
    steps = -(-reach // CHUNK)
    per_row = row_len // CHUNK
    turns = -(-steps // per_row)
    rim = 16
    halves = -(-rows // 16) * 16 + rim
    data = signal.reshape(2, rows, row_len)
    fill = rim * row_len - following.shape[1]
    edge = jnp.pad(following, ((0, 0), (0, fill))).reshape(2, rim, row_len)
    flat = taps.reshape(-1)
    spread = jnp.stack(
        [
            jnp.pad(flat, (phase * HOP, steps * CHUNK - flat.shape[0] - phase * HOP))
            for phase in range(GROUP)
        ]
    )
    chans = channels.shape[0]
    half = GROUP * chans
    places = (np.arange(chan_len)[:, None] - HOP * np.arange(GROUP)[None, :]) % chan_len
    places = jnp.asarray(places.astype(np.int32))
    turns_of = (places[:, None, :] * channels[None, :, None]).reshape(chan_len, half) % chan_len
    angles = turns_of.astype(jnp.float32) * (2.0 * math.pi / chan_len)
    rot = jnp.concatenate([jnp.cos(angles), jnp.sin(angles)], axis=1)
    rot = rot.astype(jnp.bfloat16).astype(jnp.float32)
    deep = -(-rows // 128) * 128
    shape = (len(picks), 2, width * GROUP, rows)
    return pl.pallas_call(
        functools.partial(bank_kernel, turns, per_row, picks),
        grid=(steps,),
        in_specs=[
            pl.BlockSpec((2, rows, CHUNK), lambda i: (0, 0, i % per_row)),
            pl.BlockSpec((2, rim, CHUNK), lambda i: (0, 0, i % per_row)),
            pl.BlockSpec((GROUP, CHUNK), lambda i: (0, i)),
            pl.BlockSpec((chan_len, 2 * half), lambda i: (0, 0)),
        ],
        out_specs=pl.BlockSpec(shape, lambda i: (0, 0, 0, 0)),
        out_shape=jax.ShapeDtypeStruct(shape, jnp.bfloat16),
        scratch_shapes=[
            pltpu.VMEM((2 * halves, CHUNK), jnp.bfloat16),
            pltpu.VMEM((CHUNK, 2 * half), jnp.bfloat16),
            pltpu.VMEM((turns, 2 * halves, 2 * half), jnp.float32),
            pltpu.VMEM((deep, half), jnp.float32),
        ],
        name="slot_bank",
    )(data, edge, spread, rot)


def on_device(voltages, section1_taps, section2_taps, band_starts, band_widths):
    signal = voltages[0]
    tap_count, chan_len = section1_taps.shape
    spectra = signal.shape[1] // HOP
    rim_len = tap_count * chan_len - HOP
    tm_count = lax.axis_size("tm")
    zoom_count = lax.axis_size("zoom")
    device_count = tm_count * zoom_count
    slot_count = tm_count * CH_DEV
    width = CH_DEV + 2
    following = shifted(signal[:, :rim_len], ("tm", "zoom"), -1)
    span = slot_count + 2
    band_slots = jnp.arange(-1, slot_count + 1, dtype=jnp.int32)
    channels = ((band_starts[:, None] + band_slots[None, :]) % chan_len).reshape(-1)
    picks = [tm * CH_DEV + zoom * span for tm in range(tm_count) for zoom in range(zoom_count)]
    if channels.shape[0] <= 48 and spectra % GROUP == 0:
        filled = -(-channels.shape[0] // 16) * 16
        padded = jnp.pad(channels, (0, filled - channels.shape[0]))
        packed = slot_bank(signal, following, section1_taps, padded, spectra, picks, width)
        received = lax.all_to_all(packed, ("tm", "zoom"), split_axis=0, concat_axis=0, tiled=True)
        weighted, order = phase_order(received, section2_taps, FA, FB)
    else:
        pieces = -(-chan_len // HOP)
        padded = jnp.concatenate(
            [signal, following, jnp.zeros((2, pieces * HOP), jnp.bfloat16)], axis=1
        )
        frames = weighted_frames(padded, section1_taps, spectra, HOP)
        coarse = jnp.einsum(
            "pqkn,qsn->pks", rotation_block(chan_len), frames, preferred_element_type=jnp.float32
        ).astype(jnp.bfloat16)
        wanted = np.arange(width)[:, None] + np.asarray(picks)[None, :]
        packed = jnp.take(coarse, channels[wanted.reshape(-1)], axis=1)
        packed = packed.reshape(2, width, device_count, spectra)
        received = lax.all_to_all(packed, ("tm", "zoom"), split_axis=2, concat_axis=2, tiled=True)
        series = received.reshape(2, width, -1)
        weighted, order = natural_order(series, section2_taps, FA, FB)
    spans = fine_spectra(weighted, order, KEEP, EDGE)
    slot_ids = lax.axis_index("tm") * CH_DEV + jnp.arange(CH_DEV, dtype=jnp.int32)
    band_ids = jnp.arange(band_widths.shape[0], dtype=jnp.int32)
    band_width = jnp.sum(jnp.where(band_ids == lax.axis_index("zoom"), band_widths, 0))
    upper_rim = spans[:, 2:, :, :EDGE]
    lower_rim = spans[:, :CH_DEV, :, KEEP + EDGE :]
    extended = spans[:, 1 : CH_DEV + 1]
    stitched = stitch_bands(extended, upper_rim, lower_rim, slot_ids, band_width, KEEP, EDGE)
    fine_count = stitched.shape[2]
    result = jnp.transpose(stitched, (0, 2, 1, 3)).reshape(2, fine_count, CH_DEV * KEEP)
    return result[None, None]


def solution(mesh):
    placed = (P("pol", "groups", ("tm", "zoom")), P(), P(), P("groups"), P("groups"))
    return jax.shard_map(
        on_device,
        mesh=mesh,
        in_specs=placed,
        out_specs=P("pol", "zoom", "groups", None, "tm"),
        check_vma=False,
    )
```

```python
import functools
import math

import jax
import jax.numpy as jnp
import numpy as np
from jax import lax
from jax.experimental import pallas as pl
from jax.experimental.pallas import tpu as pltpu
from jax.sharding import PartitionSpec as P

HOP = 432
FA = 27
FB = 128
KEEP = 2916
EDGE = 128
CH_DEV = 5
LIVE_DEV = 3


def shifted(value, axis, steps):
    count = lax.axis_size(axis)
    initial, last = (max(0, -steps), min(count, count - steps))
    return lax.ppermute(value, axis, [(source, source + steps) for source in range(initial, last)])


def angle_table(rows, cols, length):
    product = (
        jnp.arange(rows, dtype=jnp.int32)[:, None]
        * jnp.arange(cols, dtype=jnp.int32)[None, :]
        % length
    )
    return product.astype(jnp.float32) * (2.0 * math.pi / length)


def rotation_block(length):
    angles = angle_table(length, length, length)
    cosine_tab = jnp.cos(angles).astype(jnp.bfloat16)
    sine_tab = jnp.sin(angles).astype(jnp.bfloat16)
    return jnp.stack([jnp.stack([cosine_tab, sine_tab]), jnp.stack([-sine_tab, cosine_tab])])


def frame_view(segment, spectra, chan_len, hop_len):
    pieces = -(-chan_len // hop_len)
    framed = segment[:, : (spectra + pieces - 1) * hop_len].reshape(
        segment.shape[0], spectra + pieces - 1, hop_len
    )
    joined = jnp.concatenate(
        [framed[:, offset : offset + spectra] for offset in range(pieces)], axis=2
    )
    return joined[:, :, :chan_len]


def weighted_frames(signal, taps, spectra, hop_len):
    chan_len = taps.shape[1]
    running = jnp.zeros((2, spectra, chan_len), jnp.float32)
    for tap_index in range(taps.shape[0]):
        frames = frame_view(signal[:, tap_index * chan_len :], spectra, chan_len, hop_len)
        running = running + taps[tap_index][None, None, :] * frames.astype(jnp.float32)
    return running.astype(jnp.bfloat16)


def natural_order(series, section2_taps, radix_a, radix_b):
    tap_count, fine_len = section2_taps.shape
    items = series.shape[1]
    row_count = series.shape[2] // fine_len
    spectra = row_count - tap_count + 1
    row_blocks = series.reshape(2, items, row_count, fine_len)
    running = jnp.zeros((2, items, spectra, fine_len), jnp.float32)
    for tap_index in range(tap_count):
        running = running + section2_taps[tap_index] * row_blocks[
            :, :, tap_index : tap_index + spectra
        ].astype(jnp.float32)
    weighted = running.astype(jnp.bfloat16).reshape(2, items, spectra, radix_a, radix_b)
    return weighted, np.arange(radix_b)


def phase_order(received, section2_taps, radix_a, radix_b):
    tap_count, fine_len = section2_taps.shape
    sources, _, lines, rows = received.shape
    items = lines // GROUP
    short = fine_len // GROUP
    row_count = sources * rows // short
    spectra = row_count - tap_count + 1
    lanes = jnp.transpose(received, (1, 2, 0, 3)).reshape(2, items, GROUP, row_count, short)
    taps = jnp.transpose(section2_taps.reshape(tap_count, short, GROUP), (0, 2, 1))
    running = jnp.zeros((2, items, GROUP, spectra, short), jnp.float32)
    for tap_index in range(tap_count):
        running = running + taps[tap_index][:, None, :] * lanes[
            :, :, :, tap_index : tap_index + spectra
        ].astype(jnp.float32)
    inner = radix_b // GROUP
    weighted = running.astype(jnp.bfloat16).reshape(2, items, GROUP, spectra, radix_a, inner)
    weighted = jnp.transpose(weighted, (0, 1, 3, 4, 2, 5)).reshape(
        2, items, spectra, radix_a, radix_b
    )
    order = (np.arange(GROUP)[:, None] + GROUP * np.arange(inner)[None, :]).reshape(-1)
    return weighted, order


def ordered_angles(rows, order, length):
    product = (np.arange(rows)[:, None] * order[None, :] % length).astype(np.float32)
    return jnp.asarray(product) * (2.0 * math.pi / length)


def fine_spectra(weighted, order, keep_len, edge_len):
    _, items, spectra, radix_a, radix_b = weighted.shape
    fine_len = radix_a * radix_b
    partial_value = jnp.einsum(
        "pqkm,qcfmb->pcfkb", rotation_block(radix_a), weighted, preferred_element_type=jnp.float32
    )
    angles = ordered_angles(radix_a, order, fine_len)
    cosine_tab = jnp.cos(angles)
    sine_tab = jnp.sin(angles)
    real_part = partial_value[0] * cosine_tab + partial_value[1] * sine_tab
    imag_part = partial_value[1] * cosine_tab - partial_value[0] * sine_tab
    twiddled = jnp.concatenate([real_part, imag_part], axis=-1).astype(jnp.bfloat16)
    turned = ordered_angles(radix_b, order, radix_b).T
    cosine_b = jnp.cos(turned).astype(jnp.bfloat16)
    sine_b = jnp.sin(turned).astype(jnp.bfloat16)
    table = jnp.concatenate(
        [jnp.stack([cosine_b, -sine_b], axis=1), jnp.stack([sine_b, cosine_b], axis=1)], axis=0
    )
    spectrum = jnp.einsum(
        "cfkm,mpq->pcfqk", twiddled, table, preferred_element_type=jnp.float32
    ).reshape(2, items, spectra, fine_len)
    first = (-(keep_len // 2) - edge_len) % fine_len
    rest = keep_len + 2 * edge_len - (fine_len - first)
    return jnp.concatenate([spectrum[..., first:], spectrum[..., :rest]], axis=-1)


def stitch_bands(extended, upper_rim, lower_rim, slot_ids, band_width, keep_len, edge_len):
    centre = extended[..., edge_len : edge_len + keep_len]
    live = (slot_ids < band_width).astype(jnp.float32)[None, :, None, None]
    upper_ok = (slot_ids + 1 < band_width).astype(jnp.float32)[None, :, None, None]
    lower_ok = ((slot_ids >= 1) & (slot_ids < band_width)).astype(jnp.float32)[None, :, None, None]
    ramp = (jnp.arange(edge_len, dtype=jnp.float32) + 0.5) / (2.0 * edge_len)
    upper_weight = ramp * upper_ok
    lower_weight = ramp[::-1] * lower_ok
    low_part = centre[..., :edge_len] * (1.0 - lower_weight) + lower_rim * lower_weight
    high_part = centre[..., keep_len - edge_len :] * (1.0 - upper_weight) + upper_rim * upper_weight
    joined = jnp.concatenate(
        [low_part, centre[..., edge_len : keep_len - edge_len], high_part], axis=-1
    )
    return joined * live


GROUP = 8
CHUNK = 1152


def bank_kernel(
    turns, per_row, pick_ref, x_ref, rim_ref, taps_ref, rot_ref, out_ref, tail_ref, data, bank, total, mix, turned
):
    step = pl.program_id(0)
    rows = x_ref.shape[1]
    halves = data.shape[0] // 2
    base = halves - rim_ref.shape[1]
    half = rot_ref.shape[1] // 2
    rot_len = rot_ref.shape[0]
    piece = 128

    @pl.when(step == 0)
    def _():
        total[...] = jnp.zeros_like(total)

    for part in range(2):
        data[pl.ds(part * halves, rows), :] = x_ref[part]
        data[pl.ds(part * halves + base, halves - base), :] = rim_ref[part]

    @pl.loop(0, CHUNK // piece)
    def _(index):
        row = pl.multiple_of(index * piece, piece)
        turn = pl.multiple_of((step * CHUNK + row) % rot_len, piece)
        wide = jnp.transpose(jnp.tile(taps_ref[:, pl.ds(row, piece)], (piece // GROUP, 1)))
        for col in range(0, 2 * half, piece):
            bank[pl.ds(row, piece), pl.ds(col, piece)] = (
                wide * rot_ref[pl.ds(turn, piece), pl.ds(col, piece)]
            ).astype(jnp.bfloat16)

    total[step // per_row] += jnp.dot(data[...], bank[...], preferred_element_type=jnp.float32)

    @pl.when(step == pl.num_programs(0) - 1)
    def _():
        for shift in range(1, turns):
            for part in range(2):
                total[shift, pl.ds(part * halves + rows, shift), :] = total[
                    shift, pl.ds(part * halves + base, shift), :
                ]
        for part in range(2):
            whole = jnp.zeros((rows, half), jnp.float32)
            for shift in range(turns):
                upper = total[shift, pl.ds(shift, rows), pl.ds(part * half, half)]
                lower = total[shift, pl.ds(halves + shift, rows), pl.ds((1 - part) * half, half)]
                whole += upper + lower if part == 0 else lower - upper
            mix[pl.ds(0, rows), pl.ds(0, half)] = whole
            turned[part] = jnp.transpose(mix[...])[:half]
        dests, lines, main = out_ref.shape
        width = lines // (2 * GROUP)
        fill = -(-lines // 128) * 128 - lines

        @pl.loop(0, dests)
        def _(dest):
            blocks = []
            for part in range(2):
                for slot in range(width):
                    line = pl.multiple_of(pick_ref[dest * width + slot] * GROUP, GROUP)
                    blocks.append(turned[part, pl.ds(line, GROUP), :])
            block = jnp.concatenate(blocks, axis=0)
            out_ref[dest] = block[:, :main].astype(jnp.bfloat16)
            spare = jnp.zeros((fill, turned.shape[2] - main), jnp.float32)
            rest = jnp.transpose(jnp.concatenate([block[:, main:], spare], axis=0))
            tail_ref[dest] = rest[: tail_ref.shape[1], :lines].astype(jnp.bfloat16)


def slot_bank(signal, following, taps, channels, spectra, picks):
    tap_count, chan_len = taps.shape
    row_len = GROUP * HOP
    rows = spectra // GROUP
    reach = (GROUP - 1) * HOP + tap_count * chan_len
    steps = -(-reach // CHUNK)
    per_row = row_len // CHUNK
    turns = -(-steps // per_row)
    rim = 16
    halves = -(-rows // 16) * 16 + rim
    data = signal.reshape(2, rows, row_len)
    fill = rim * row_len - following.shape[1]
    edge = jnp.pad(following, ((0, 0), (0, fill))).reshape(2, rim, row_len)
    flat = taps.reshape(-1)
    spread = jnp.stack(
        [
            jnp.pad(flat, (phase * HOP, steps * CHUNK - flat.shape[0] - phase * HOP))
            for phase in range(GROUP)
        ]
    )
    chans = channels.shape[0]
    half = GROUP * chans
    places = (np.arange(chan_len)[:, None] - HOP * np.arange(GROUP)[None, :]) % chan_len
    places = jnp.asarray(places.astype(np.int32))
    turns_of = (places[:, None, :] * channels[None, :, None]).reshape(chan_len, half) % chan_len
    angles = turns_of.astype(jnp.float32) * (2.0 * math.pi / chan_len)
    rot = jnp.concatenate([jnp.cos(angles), jnp.sin(angles)], axis=1)
    rot = rot.astype(jnp.bfloat16).astype(jnp.float32)
    deep = -(-rows // 128) * 128
    wide = -(-half // 128) * 128
    main = rows // 128 * 128
    lines = 2 * picks.shape[1] * GROUP
    shape = (picks.shape[0], lines, main)
    tail = (picks.shape[0], -(-(rows - main) // 16) * 16, lines)
    return pl.pallas_call(
        functools.partial(bank_kernel, turns, per_row),
        out_shape=(
            jax.ShapeDtypeStruct(shape, jnp.bfloat16),
            jax.ShapeDtypeStruct(tail, jnp.bfloat16),
        ),
        grid_spec=pltpu.PrefetchScalarGridSpec(
            num_scalar_prefetch=1,
            grid=(steps,),
            in_specs=[
                pl.BlockSpec((2, rows, CHUNK), lambda i, p: (0, 0, i % per_row)),
                pl.BlockSpec((2, rim, CHUNK), lambda i, p: (0, 0, i % per_row)),
                pl.BlockSpec((GROUP, CHUNK), lambda i, p: (0, i)),
                pl.BlockSpec((chan_len, 2 * half), lambda i, p: (0, 0)),
            ],
            out_specs=(
                pl.BlockSpec(shape, lambda i, p: (0, 0, 0)),
                pl.BlockSpec(tail, lambda i, p: (0, 0, 0)),
            ),
            scratch_shapes=[
            pltpu.VMEM((2 * halves, CHUNK), jnp.bfloat16),
            pltpu.VMEM((CHUNK, 2 * half), jnp.bfloat16),
            pltpu.VMEM((turns, 2 * halves, 2 * half), jnp.float32),
            pltpu.VMEM((deep, wide), jnp.float32),
            pltpu.VMEM((2, half, deep), jnp.float32),
            ],
        ),
        name="slot_bank",
    )(picks.reshape(-1), data, edge, spread, rot)


def swap_kernel(zooms, in_ref, in_tail, out_ref, out_tail, send_sems, recv_sems):
    count = in_ref.shape[0]
    me = lax.axis_index("tm") * zooms + lax.axis_index("zoom")
    barrier = pltpu.get_barrier_semaphore()

    def place(step):
        other = lax.rem(me + step, count)
        return other, {"tm": other // zooms, "zoom": lax.rem(other, zooms)}

    for step in range(1, count):
        pl.semaphore_signal(
            barrier, inc=1, device_id=place(step)[1], device_id_type=pl.DeviceIdType.MESH
        )
    pl.semaphore_wait(barrier, count - 1)
    copies = []
    for step in range(1, count):
        other, where = place(step)
        for which, (source, target) in enumerate(((in_ref, out_ref), (in_tail, out_tail))):
            copy = pltpu.make_async_remote_copy(
                src_ref=source.at[other],
                dst_ref=target.at[me],
                send_sem=send_sems.at[which, step],
                recv_sem=recv_sems.at[which, step],
                device_id=where,
                device_id_type=pl.DeviceIdType.MESH,
            )
            copy.start()
            copies.append(copy)
    out_ref[me] = in_ref[me]
    out_tail[me] = in_tail[me]
    for copy in copies:
        copy.wait()


def swapped(packed, tail, zooms, rows):
    count, lines, main = packed.shape
    body, rest = pl.pallas_call(
        functools.partial(swap_kernel, zooms),
        out_shape=tuple(jax.ShapeDtypeStruct(x.shape, x.dtype) for x in (packed, tail)),
        in_specs=[pl.BlockSpec(memory_space=pltpu.VMEM)] * 2,
        out_specs=(pl.BlockSpec(memory_space=pltpu.VMEM),) * 2,
        scratch_shapes=[
            pltpu.SemaphoreType.DMA((2, count)),
            pltpu.SemaphoreType.DMA((2, count)),
        ],
        compiler_params=pltpu.CompilerParams(collective_id=0, has_side_effects=True),
        name="swap_slots",
    )(packed, tail)
    rest = jnp.transpose(rest, (0, 2, 1))[:, :, : rows - main]
    return jnp.concatenate([body, rest], axis=2).reshape(count, 2, lines // 2, rows)


def on_device(voltages, section1_taps, section2_taps, band_starts, band_widths):
    signal = voltages[0]
    tap_count, chan_len = section1_taps.shape
    spectra = signal.shape[1] // HOP
    rim_len = tap_count * chan_len - HOP
    tm_count = lax.axis_size("tm")
    zoom_count = lax.axis_size("zoom")
    device_count = tm_count * zoom_count
    slot_count = tm_count * CH_DEV
    width = CH_DEV + 2
    following = shifted(signal[:, :rim_len], ("tm", "zoom"), -1)
    span = slot_count + 2
    band_slots = jnp.arange(-1, slot_count + 1, dtype=jnp.int32)
    channels = ((band_starts[:, None] + band_slots[None, :]) % chan_len).reshape(-1)
    picks = [tm * CH_DEV + zoom * span for tm in range(tm_count) for zoom in range(zoom_count)]
    live_count = LIVE_DEV * device_count
    ragged = spectra // GROUP % 128
    if live_count <= 48 and spectra % GROUP == 0 and spectra // GROUP > 128 and ragged:
        band_ends = jnp.cumsum(band_widths)
        band_firsts = band_ends - band_widths
        live_ids = jnp.arange(live_count, dtype=jnp.int32)
        band_of = jnp.sum((band_ends[None, :] <= live_ids[:, None]).astype(jnp.int32), axis=1)
        member = band_of[:, None] == jnp.arange(zoom_count, dtype=jnp.int32)[None, :]
        shifts = jnp.where(member, (band_starts - band_firsts)[None, :], 0)
        channels = (jnp.sum(shifts, axis=1) + live_ids) % chan_len
        slots = np.arange(tm_count)[:, None, None] * CH_DEV + np.arange(-1, CH_DEV + 1)
        slots = jnp.asarray(slots.astype(np.int32)) + band_firsts[None, :, None]
        lines = jnp.clip(slots, 0, live_count - 1).reshape(device_count, width)
        packed, tail = slot_bank(signal, following, section1_taps, channels, spectra, lines)
        received = swapped(packed, tail, zoom_count, spectra // GROUP)
        weighted, order = phase_order(received, section2_taps, FA, FB)
    else:
        pieces = -(-chan_len // HOP)
        padded = jnp.concatenate(
            [signal, following, jnp.zeros((2, pieces * HOP), jnp.bfloat16)], axis=1
        )
        frames = weighted_frames(padded, section1_taps, spectra, HOP)
        coarse = jnp.einsum(
            "pqkn,qsn->pks", rotation_block(chan_len), frames, preferred_element_type=jnp.float32
        ).astype(jnp.bfloat16)
        wanted = np.arange(width)[:, None] + np.asarray(picks)[None, :]
        packed = jnp.take(coarse, channels[wanted.reshape(-1)], axis=1)
        packed = packed.reshape(2, width, device_count, spectra)
        received = lax.all_to_all(packed, ("tm", "zoom"), split_axis=2, concat_axis=2, tiled=True)
        series = received.reshape(2, width, -1)
        weighted, order = natural_order(series, section2_taps, FA, FB)
    spans = fine_spectra(weighted, order, KEEP, EDGE)
    slot_ids = lax.axis_index("tm") * CH_DEV + jnp.arange(CH_DEV, dtype=jnp.int32)
    band_ids = jnp.arange(band_widths.shape[0], dtype=jnp.int32)
    band_width = jnp.sum(jnp.where(band_ids == lax.axis_index("zoom"), band_widths, 0))
    upper_rim = spans[:, 2:, :, :EDGE]
    lower_rim = spans[:, :CH_DEV, :, KEEP + EDGE :]
    extended = spans[:, 1 : CH_DEV + 1]
    stitched = stitch_bands(extended, upper_rim, lower_rim, slot_ids, band_width, KEEP, EDGE)
    fine_count = stitched.shape[2]
    result = jnp.transpose(stitched, (0, 2, 1, 3)).reshape(2, fine_count, CH_DEV * KEEP)
    return result[None, None]


def solution(mesh):
    placed = (P("pol", "groups", ("tm", "zoom")), P(), P(), P("groups"), P("groups"))
    return jax.shard_map(
        on_device,
        mesh=mesh,
        in_specs=placed,
        out_specs=P("pol", "zoom", "groups", None, "tm"),
        check_vma=False,
    )
```

```python
import functools
import math

import jax
import jax.numpy as jnp
import numpy as np
from jax import lax
from jax.experimental import pallas as pl
from jax.experimental.pallas import tpu as pltpu
from jax.sharding import PartitionSpec as P

HOP = 432
FA = 27
FB = 128
KEEP = 2916
EDGE = 128
CH_DEV = 5
LIVE_DEV = 3


def shifted(value, axis, steps):
    count = lax.axis_size(axis)
    initial, last = (max(0, -steps), min(count, count - steps))
    return lax.ppermute(value, axis, [(source, source + steps) for source in range(initial, last)])


def angle_table(rows, cols, length):
    product = (
        jnp.arange(rows, dtype=jnp.int32)[:, None]
        * jnp.arange(cols, dtype=jnp.int32)[None, :]
        % length
    )
    return product.astype(jnp.float32) * (2.0 * math.pi / length)


def rotation_block(length):
    angles = angle_table(length, length, length)
    cosine_tab = jnp.cos(angles).astype(jnp.bfloat16)
    sine_tab = jnp.sin(angles).astype(jnp.bfloat16)
    return jnp.stack([jnp.stack([cosine_tab, sine_tab]), jnp.stack([-sine_tab, cosine_tab])])


def frame_view(segment, spectra, chan_len, hop_len):
    pieces = -(-chan_len // hop_len)
    framed = segment[:, : (spectra + pieces - 1) * hop_len].reshape(
        segment.shape[0], spectra + pieces - 1, hop_len
    )
    joined = jnp.concatenate(
        [framed[:, offset : offset + spectra] for offset in range(pieces)], axis=2
    )
    return joined[:, :, :chan_len]


def weighted_frames(signal, taps, spectra, hop_len):
    chan_len = taps.shape[1]
    running = jnp.zeros((2, spectra, chan_len), jnp.float32)
    for tap_index in range(taps.shape[0]):
        frames = frame_view(signal[:, tap_index * chan_len :], spectra, chan_len, hop_len)
        running = running + taps[tap_index][None, None, :] * frames.astype(jnp.float32)
    return running.astype(jnp.bfloat16)


def natural_order(series, section2_taps, radix_a, radix_b):
    tap_count, fine_len = section2_taps.shape
    items = series.shape[1]
    row_count = series.shape[2] // fine_len
    spectra = row_count - tap_count + 1
    row_blocks = series.reshape(2, items, row_count, fine_len)
    running = jnp.zeros((2, items, spectra, fine_len), jnp.float32)
    for tap_index in range(tap_count):
        running = running + section2_taps[tap_index] * row_blocks[
            :, :, tap_index : tap_index + spectra
        ].astype(jnp.float32)
    weighted = running.astype(jnp.bfloat16).reshape(2, items, spectra, radix_a, radix_b)
    return weighted, np.arange(radix_b)


def phase_order(received, section2_taps, radix_a, radix_b):
    tap_count, fine_len = section2_taps.shape
    sources, _, lines, rows = received.shape
    items = lines // GROUP
    short = fine_len // GROUP
    row_count = sources * rows // short
    spectra = row_count - tap_count + 1
    lanes = jnp.transpose(received, (1, 2, 0, 3)).reshape(2, items, GROUP, row_count, short)
    taps = jnp.transpose(section2_taps.reshape(tap_count, short, GROUP), (0, 2, 1))
    running = jnp.zeros((2, items, GROUP, spectra, short), jnp.float32)
    for tap_index in range(tap_count):
        running = running + taps[tap_index][:, None, :] * lanes[
            :, :, :, tap_index : tap_index + spectra
        ].astype(jnp.float32)
    inner = radix_b // GROUP
    weighted = running.astype(jnp.bfloat16).reshape(2, items, GROUP, spectra, radix_a, inner)
    weighted = jnp.transpose(weighted, (0, 1, 3, 4, 2, 5)).reshape(
        2, items, spectra, radix_a, radix_b
    )
    order = (np.arange(GROUP)[:, None] + GROUP * np.arange(inner)[None, :]).reshape(-1)
    return weighted, order


def ordered_angles(rows, order, length):
    product = (np.arange(rows)[:, None] * order[None, :] % length).astype(np.float32)
    return jnp.asarray(product) * (2.0 * math.pi / length)


def fine_spectra(weighted, order, keep_len, edge_len):
    _, items, spectra, radix_a, radix_b = weighted.shape
    fine_len = radix_a * radix_b
    partial_value = jnp.einsum(
        "pqkm,qcfmb->pcfkb", rotation_block(radix_a), weighted, preferred_element_type=jnp.float32
    )
    angles = ordered_angles(radix_a, order, fine_len)
    cosine_tab = jnp.cos(angles)
    sine_tab = jnp.sin(angles)
    real_part = partial_value[0] * cosine_tab + partial_value[1] * sine_tab
    imag_part = partial_value[1] * cosine_tab - partial_value[0] * sine_tab
    twiddled = jnp.concatenate([real_part, imag_part], axis=-1).astype(jnp.bfloat16)
    turned = ordered_angles(radix_b, order, radix_b).T
    cosine_b = jnp.cos(turned).astype(jnp.bfloat16)
    sine_b = jnp.sin(turned).astype(jnp.bfloat16)
    table = jnp.concatenate(
        [jnp.stack([cosine_b, -sine_b], axis=1), jnp.stack([sine_b, cosine_b], axis=1)], axis=0
    )
    spectrum = jnp.einsum(
        "cfkm,mpq->pcfqk", twiddled, table, preferred_element_type=jnp.float32
    ).reshape(2, items, spectra, fine_len)
    first = (-(keep_len // 2) - edge_len) % fine_len
    rest = keep_len + 2 * edge_len - (fine_len - first)
    return jnp.concatenate([spectrum[..., first:], spectrum[..., :rest]], axis=-1)


def stitch_bands(extended, upper_rim, lower_rim, slot_ids, band_width, keep_len, edge_len):
    centre = extended[..., edge_len : edge_len + keep_len]
    live = (slot_ids < band_width).astype(jnp.float32)[None, :, None, None]
    upper_ok = (slot_ids + 1 < band_width).astype(jnp.float32)[None, :, None, None]
    lower_ok = ((slot_ids >= 1) & (slot_ids < band_width)).astype(jnp.float32)[None, :, None, None]
    ramp = (jnp.arange(edge_len, dtype=jnp.float32) + 0.5) / (2.0 * edge_len)
    upper_weight = ramp * upper_ok
    lower_weight = ramp[::-1] * lower_ok
    low_part = centre[..., :edge_len] * (1.0 - lower_weight) + lower_rim * lower_weight
    high_part = centre[..., keep_len - edge_len :] * (1.0 - upper_weight) + upper_rim * upper_weight
    joined = jnp.concatenate(
        [low_part, centre[..., edge_len : keep_len - edge_len], high_part], axis=-1
    )
    return joined * live


GROUP = 8
CHUNK = 1152


def bank_kernel(
    turns, per_row, pick_ref, x_ref, rim_ref, taps_ref, rot_ref, out_ref, tail_ref, data, bank, total, mix, turned
):
    step = pl.program_id(0)
    rows = x_ref.shape[1]
    halves = data.shape[1] // 2
    base = halves - rim_ref.shape[1]
    half = rot_ref.shape[1] // 2
    rot_len = rot_ref.shape[0]
    piece = 128

    @pl.when(step == 0)
    def _():
        total[...] = jnp.zeros_like(total)

    @pl.when(step < per_row)
    def _():
        for part in range(2):
            data[step, pl.ds(part * halves, rows), :] = x_ref[part]
            data[step, pl.ds(part * halves + base, halves - base), :] = rim_ref[part]

    @pl.loop(0, CHUNK // piece)
    def _(index):
        row = pl.multiple_of(index * piece, piece)
        turn = pl.multiple_of((step * CHUNK + row) % rot_len, piece)
        wide = jnp.transpose(jnp.tile(taps_ref[:, pl.ds(row, piece)], (piece // GROUP, 1)))
        for col in range(0, 2 * half, piece):
            bank[pl.ds(row, piece), pl.ds(col, piece)] = (
                wide * rot_ref[pl.ds(turn, piece), pl.ds(col, piece)]
            ).astype(jnp.bfloat16)

    total[step // per_row] += jnp.dot(
        data[step % per_row], bank[...], preferred_element_type=jnp.float32
    )

    @pl.when(step == pl.num_programs(0) - 1)
    def _():
        for shift in range(1, turns):
            for part in range(2):
                total[shift, pl.ds(part * halves + rows, shift), :] = total[
                    shift, pl.ds(part * halves + base, shift), :
                ]
        for part in range(2):
            whole = jnp.zeros((rows, half), jnp.float32)
            for shift in range(turns):
                upper = total[shift, pl.ds(shift, rows), pl.ds(part * half, half)]
                lower = total[shift, pl.ds(halves + shift, rows), pl.ds((1 - part) * half, half)]
                whole += upper + lower if part == 0 else lower - upper
            mix[pl.ds(0, rows), pl.ds(0, half)] = whole
            turned[part] = jnp.transpose(mix[...])[:half]
        dests, lines, main = out_ref.shape
        width = lines // (2 * GROUP)
        fill = -(-lines // 128) * 128 - lines

        @pl.loop(0, dests)
        def _(dest):
            blocks = []
            for part in range(2):
                for slot in range(width):
                    line = pl.multiple_of(pick_ref[dest * width + slot] * GROUP, GROUP)
                    blocks.append(turned[part, pl.ds(line, GROUP), :])
            block = jnp.concatenate(blocks, axis=0)
            out_ref[dest] = block[:, :main].astype(jnp.bfloat16)
            spare = jnp.zeros((fill, turned.shape[2] - main), jnp.float32)
            rest = jnp.transpose(jnp.concatenate([block[:, main:], spare], axis=0))
            tail_ref[dest] = rest[: tail_ref.shape[1], :lines].astype(jnp.bfloat16)


def slot_bank(signal, following, taps, channels, spectra, picks):
    tap_count, chan_len = taps.shape
    row_len = GROUP * HOP
    rows = spectra // GROUP
    reach = (GROUP - 1) * HOP + tap_count * chan_len
    steps = -(-reach // CHUNK)
    per_row = row_len // CHUNK
    turns = -(-steps // per_row)
    rim = 16
    halves = -(-rows // 16) * 16 + rim
    data = signal.reshape(2, rows, row_len)
    fill = rim * row_len - following.shape[1]
    edge = jnp.pad(following, ((0, 0), (0, fill))).reshape(2, rim, row_len)
    flat = taps.reshape(-1)
    spread = jnp.stack(
        [
            jnp.pad(flat, (phase * HOP, steps * CHUNK - flat.shape[0] - phase * HOP))
            for phase in range(GROUP)
        ]
    )
    chans = channels.shape[0]
    half = GROUP * chans
    places = (np.arange(chan_len)[:, None] - HOP * np.arange(GROUP)[None, :]) % chan_len
    places = jnp.asarray(places.astype(np.int32))
    turns_of = (places[:, None, :] * channels[None, :, None]).reshape(chan_len, half) % chan_len
    angles = turns_of.astype(jnp.float32) * (2.0 * math.pi / chan_len)
    rot = jnp.concatenate([jnp.cos(angles), jnp.sin(angles)], axis=1)
    rot = rot.astype(jnp.bfloat16).astype(jnp.float32)
    deep = -(-rows // 128) * 128
    wide = -(-half // 128) * 128
    main = rows // 128 * 128
    lines = 2 * picks.shape[1] * GROUP
    shape = (picks.shape[0], lines, main)
    tail = (picks.shape[0], -(-(rows - main) // 16) * 16, lines)
    return pl.pallas_call(
        functools.partial(bank_kernel, turns, per_row),
        out_shape=(
            jax.ShapeDtypeStruct(shape, jnp.bfloat16),
            jax.ShapeDtypeStruct(tail, jnp.bfloat16),
        ),
        grid_spec=pltpu.PrefetchScalarGridSpec(
            num_scalar_prefetch=1,
            grid=(steps,),
            in_specs=[
                pl.BlockSpec((2, rows, CHUNK), lambda i, p: (0, 0, jnp.minimum(i, per_row - 1))),
                pl.BlockSpec((2, rim, CHUNK), lambda i, p: (0, 0, jnp.minimum(i, per_row - 1))),
                pl.BlockSpec((GROUP, CHUNK), lambda i, p: (0, i)),
                pl.BlockSpec((chan_len, 2 * half), lambda i, p: (0, 0)),
            ],
            out_specs=(
                pl.BlockSpec(shape, lambda i, p: (0, 0, 0)),
                pl.BlockSpec(tail, lambda i, p: (0, 0, 0)),
            ),
            scratch_shapes=[
            pltpu.VMEM((per_row, 2 * halves, CHUNK), jnp.bfloat16),
            pltpu.VMEM((CHUNK, 2 * half), jnp.bfloat16),
            pltpu.VMEM((turns, 2 * halves, 2 * half), jnp.float32),
            pltpu.VMEM((deep, wide), jnp.float32),
            pltpu.VMEM((2, half, deep), jnp.float32),
            ],
        ),
        name="slot_bank",
    )(picks.reshape(-1), data, edge, spread, rot)


def swap_kernel(zooms, in_ref, in_tail, out_ref, out_tail, send_sems, recv_sems):
    count = in_ref.shape[0]
    me = lax.axis_index("tm") * zooms + lax.axis_index("zoom")
    barrier = pltpu.get_barrier_semaphore()

    def place(step):
        other = lax.rem(me + step, count)
        return other, {"tm": other // zooms, "zoom": lax.rem(other, zooms)}

    for step in range(1, count):
        pl.semaphore_signal(
            barrier, inc=1, device_id=place(step)[1], device_id_type=pl.DeviceIdType.MESH
        )
    pl.semaphore_wait(barrier, count - 1)
    copies = []
    for step in range(1, count):
        other, where = place(step)
        for which, (source, target) in enumerate(((in_ref, out_ref), (in_tail, out_tail))):
            copy = pltpu.make_async_remote_copy(
                src_ref=source.at[other],
                dst_ref=target.at[me],
                send_sem=send_sems.at[which, step],
                recv_sem=recv_sems.at[which, step],
                device_id=where,
                device_id_type=pl.DeviceIdType.MESH,
            )
            copy.start()
            copies.append(copy)
    out_ref[me] = in_ref[me]
    out_tail[me] = in_tail[me]
    for copy in copies:
        copy.wait()


def swapped(packed, tail, zooms, rows):
    count, lines, main = packed.shape
    body, rest = pl.pallas_call(
        functools.partial(swap_kernel, zooms),
        out_shape=tuple(jax.ShapeDtypeStruct(x.shape, x.dtype) for x in (packed, tail)),
        in_specs=[pl.BlockSpec(memory_space=pltpu.VMEM)] * 2,
        out_specs=(pl.BlockSpec(memory_space=pltpu.VMEM),) * 2,
        scratch_shapes=[
            pltpu.SemaphoreType.DMA((2, count)),
            pltpu.SemaphoreType.DMA((2, count)),
        ],
        compiler_params=pltpu.CompilerParams(collective_id=0, has_side_effects=True),
        name="swap_slots",
    )(packed, tail)
    rest = jnp.transpose(rest, (0, 2, 1))[:, :, : rows - main]
    return jnp.concatenate([body, rest], axis=2).reshape(count, 2, lines // 2, rows)


def on_device(voltages, section1_taps, section2_taps, band_starts, band_widths):
    signal = voltages[0]
    tap_count, chan_len = section1_taps.shape
    spectra = signal.shape[1] // HOP
    rim_len = tap_count * chan_len - HOP
    tm_count = lax.axis_size("tm")
    zoom_count = lax.axis_size("zoom")
    device_count = tm_count * zoom_count
    slot_count = tm_count * CH_DEV
    width = CH_DEV + 2
    following = shifted(signal[:, :rim_len], ("tm", "zoom"), -1)
    span = slot_count + 2
    band_slots = jnp.arange(-1, slot_count + 1, dtype=jnp.int32)
    channels = ((band_starts[:, None] + band_slots[None, :]) % chan_len).reshape(-1)
    picks = [tm * CH_DEV + zoom * span for tm in range(tm_count) for zoom in range(zoom_count)]
    live_count = LIVE_DEV * device_count
    ragged = spectra // GROUP % 128
    if live_count <= 48 and spectra % GROUP == 0 and spectra // GROUP > 128 and ragged:
        band_ends = jnp.cumsum(band_widths)
        band_firsts = band_ends - band_widths
        live_ids = jnp.arange(live_count, dtype=jnp.int32)
        band_of = jnp.sum((band_ends[None, :] <= live_ids[:, None]).astype(jnp.int32), axis=1)
        member = band_of[:, None] == jnp.arange(zoom_count, dtype=jnp.int32)[None, :]
        shifts = jnp.where(member, (band_starts - band_firsts)[None, :], 0)
        channels = (jnp.sum(shifts, axis=1) + live_ids) % chan_len
        slots = np.arange(tm_count)[:, None, None] * CH_DEV + np.arange(-1, CH_DEV + 1)
        slots = jnp.asarray(slots.astype(np.int32)) + band_firsts[None, :, None]
        lines = jnp.clip(slots, 0, live_count - 1).reshape(device_count, width)
        packed, tail = slot_bank(signal, following, section1_taps, channels, spectra, lines)
        received = swapped(packed, tail, zoom_count, spectra // GROUP)
        weighted, order = phase_order(received, section2_taps, FA, FB)
    else:
        pieces = -(-chan_len // HOP)
        padded = jnp.concatenate(
            [signal, following, jnp.zeros((2, pieces * HOP), jnp.bfloat16)], axis=1
        )
        frames = weighted_frames(padded, section1_taps, spectra, HOP)
        coarse = jnp.einsum(
            "pqkn,qsn->pks", rotation_block(chan_len), frames, preferred_element_type=jnp.float32
        ).astype(jnp.bfloat16)
        wanted = np.arange(width)[:, None] + np.asarray(picks)[None, :]
        packed = jnp.take(coarse, channels[wanted.reshape(-1)], axis=1)
        packed = packed.reshape(2, width, device_count, spectra)
        received = lax.all_to_all(packed, ("tm", "zoom"), split_axis=2, concat_axis=2, tiled=True)
        series = received.reshape(2, width, -1)
        weighted, order = natural_order(series, section2_taps, FA, FB)
    spans = fine_spectra(weighted, order, KEEP, EDGE)
    slot_ids = lax.axis_index("tm") * CH_DEV + jnp.arange(CH_DEV, dtype=jnp.int32)
    band_ids = jnp.arange(band_widths.shape[0], dtype=jnp.int32)
    band_width = jnp.sum(jnp.where(band_ids == lax.axis_index("zoom"), band_widths, 0))
    upper_rim = spans[:, 2:, :, :EDGE]
    lower_rim = spans[:, :CH_DEV, :, KEEP + EDGE :]
    extended = spans[:, 1 : CH_DEV + 1]
    stitched = stitch_bands(extended, upper_rim, lower_rim, slot_ids, band_width, KEEP, EDGE)
    fine_count = stitched.shape[2]
    result = jnp.transpose(stitched, (0, 2, 1, 3)).reshape(2, fine_count, CH_DEV * KEEP)
    return result[None, None]


def solution(mesh):
    placed = (P("pol", "groups", ("tm", "zoom")), P(), P(), P("groups"), P("groups"))
    return jax.shard_map(
        on_device,
        mesh=mesh,
        in_specs=placed,
        out_specs=P("pol", "zoom", "groups", None, "tm"),
        check_vma=False,
    )
```
